512 devices in a mesh: row: 32 (over x, z), col: 16 (over y, core).
Axes of the slice: x: 4, y: 8, z: 8, core: 2. Of those that a mesh axis runs over, the one named last changes fastest.
Arguments:
- c_matrix: float32 [12288, 12288], P('row', 'col'), may hold values from -6 to 6
- a_upper: bfloat16 [12288, 12288], P('row', 'col'), may hold values from -0.3125 to 0.3125
- b_upper: bfloat16 [12288, 12288], P('row', 'col'), may hold values from -0.3125 to 0.3125
- a_vectors: bfloat16 [12288, 384], P('row'), may hold values from -1 to 2, as said below
- a_inverse: bfloat16 [12288, 384], P('row'), may hold values from -1 to 2, as said below
- b_vectors: bfloat16 [12288, 384], P('row'), may hold values from -1 to 2, as said below
- b_inverse: bfloat16 [12288, 384], P('row'), may hold values from -1 to 2, as said below
- a_values: bfloat16 [12288], P('row'), may hold values from 0.5 to 4
- b_values: bfloat16 [12288], P('row'), may hold values from 0.5 to 4
Outputs:
- overwritten: float32 [12288, 12288], P('row', 'col')
The draws below stay inside these ranges and needn't reach their ends.
Inputs may be any that keep to these rules, and one draw needn't show every extreme that they name: `a_vectors`: each 384 x 384 tile is an identity matrix plus independent entries of deviation about 0.5 / sqrt(384). `a_inverse`: each 384 x 384 tile is an identity matrix plus independent entries of deviation about 0.5 / sqrt(384). `b_vectors`: each 384 x 384 tile is an identity matrix plus independent entries of deviation about 0.5 / sqrt(384). `b_inverse`: each 384 x 384 tile is an identity matrix plus independent entries of deviation about 0.5 / sqrt(384).
All inputs are finite; a program needn't handle non-finite values.
Results may differ from the reference program's by a relative error of at most 0.012.
Values may be sent and summed in bfloat16 or wider, within the bound.
No kernel may reach another device: no remote copies, remote signals or barrier semaphores. Data moves between devices by JAX's collectives and lax.ppermute only.
A program may use at most 64 MiB of HBM per device.

```python
import math
import jax
import jax.numpy as jnp

TILE = 384
WAVES = 3
W = 12288


def eigen_tiles(key):
    blocks = W // TILE
    jitter = jnp.clip(jax.random.normal(key, (W, TILE), jnp.float32), -4.0, 4.0)
    identity = jnp.tile(jnp.eye(TILE, dtype=jnp.float32), (blocks, 1))
    return (identity + 0.5 * jitter / math.sqrt(TILE)).astype(jnp.bfloat16)


def draw_a_vectors(key, part):
    return eigen_tiles(jax.random.fold_in(key, 11))


def draw_a_inverse(key, part):
    return eigen_tiles(jax.random.fold_in(key, 23))


def draw_b_vectors(key, part):
    return eigen_tiles(jax.random.fold_in(key, 37))


def draw_b_inverse(key, part):
    return eigen_tiles(jax.random.fold_in(key, 41))


def steps_of(stream_key, dims, cuts, smallest, largest):
    def one(position, parts):
        draws = jax.random.uniform(jax.random.fold_in(jax.random.fold_in(stream_key, 6), position), (parts,), jnp.float32, smallest / len(cuts), largest / len(cuts))
        return jnp.repeat(jnp.exp(draws), dims[position] // parts).reshape((-1,) + (1,) * (len(dims) - position - 1))

    gain = one(*cuts[0])
    for cut in cuts[1:]:
        gain = gain * one(*cut)
    return gain


def centred(rng, extent, width, limit, cuts=(), kind=jnp.bfloat16):
    drawn = jax.random.normal(rng, extent, jnp.float32) * width
    if len(cuts) > 0:
        drawn = steps_of(rng, extent, cuts, -0.22, 0.18) * drawn
    return jnp.clip(drawn, min=-limit, max=limit).astype(kind)


def setup_inputs(seed: int = 0) -> dict:
    streams_of = jax.random.split(jax.random.key(seed), 10)
    c_matrix = centred(streams_of[0], (W, W), 1.0, 6.0, ((0, 32), (1, 16)), jnp.float32)
    a_upper = centred(streams_of[1], (W, W), TILE ** -0.5, 0.3125, ((0, 32), (1, 16)))
    b_upper = centred(streams_of[2], (W, W), TILE ** -0.5, 0.3125, ((0, 32), (1, 16)))
    a_vectors = draw_a_vectors(jax.random.fold_in(streams_of[9], 71), 0)
    a_inverse = draw_a_inverse(jax.random.fold_in(streams_of[9], 71), 0)
    b_vectors = draw_b_vectors(jax.random.fold_in(streams_of[9], 71), 0)
    b_inverse = draw_b_inverse(jax.random.fold_in(streams_of[9], 71), 0)
    a_values = jnp.clip(jnp.exp(math.log(4.0) - 2.0794415 * jax.random.uniform(streams_of[7], (W,), jnp.float32) ** steps_of(streams_of[7], (W,), ((0, 32),), -0.2, 0.2)), 0.5, 4.0).astype(jnp.bfloat16)
    b_values = jnp.clip(jnp.exp(math.log(4.0) - 2.0794415 * jax.random.uniform(streams_of[8], (W,), jnp.float32) ** steps_of(streams_of[8], (W,), ((0, 32),), -0.2, 0.2)), 0.5, 4.0).astype(jnp.bfloat16)
    return dict(c_matrix=c_matrix, a_upper=a_upper, b_upper=b_upper, a_vectors=a_vectors, a_inverse=a_inverse, b_vectors=b_vectors, b_inverse=b_inverse, a_values=a_values, b_values=b_values)


def batch_product(form, left, right):
    return jnp.einsum(form, left.astype(jnp.float32), right.astype(jnp.float32))


def reference(c_matrix, a_upper, b_upper, a_vectors, a_inverse, b_vectors, b_inverse, a_values, b_values):
    blocks = W // TILE
    state_tiles = c_matrix.reshape(blocks, TILE, blocks, TILE)
    left_vectors = a_vectors.reshape(blocks, TILE, TILE)
    left_inverse = a_inverse.reshape(blocks, TILE, TILE)
    right_vectors = b_vectors.reshape(blocks, TILE, TILE)
    right_inverse = b_inverse.reshape(blocks, TILE, TILE)
    left_values = a_values.reshape(blocks, TILE).astype(jnp.float32)
    right_values = b_values.reshape(blocks, TILE).astype(jnp.float32)
    tile_ids = jnp.arange(blocks).astype(jnp.int32)
    for offset in range(WAVES - 1, -1, -1):
        wave_count = blocks - offset
        col_index = jnp.arange(wave_count).astype(jnp.int32)
        row_index = col_index + offset
        residue = state_tiles[row_index, :, col_index, :]
        section_one = batch_product('jab,jbc->jac', left_inverse[row_index], residue.astype(jnp.bfloat16)).astype(jnp.bfloat16)
        second = batch_product('jab,jbc->jac', section_one, right_vectors[col_index])
        divisor = left_values[row_index][:, :, None] + right_values[col_index][:, None, :]
        scaled = (second / divisor).astype(jnp.bfloat16)
        section_three = batch_product('jab,jbc->jac', left_vectors[row_index], scaled).astype(jnp.bfloat16)
        solved = batch_product('jab,jbc->jac', section_three, right_inverse[col_index])
        state_tiles = state_tiles.at[row_index, :, col_index, :].set(solved)
        packed = solved.astype(jnp.bfloat16)
        a_columns = a_upper.reshape(W, blocks, TILE)[:, offset:, :]
        change = batch_product('kjt,jtu->jku', a_columns, packed).reshape(wave_count, blocks, TILE, TILE)
        keep_mask = tile_ids[None, :] < row_index[:, None]
        change = jnp.where(keep_mask[:, :, None, None], change, jnp.float32(0.0))
        state_tiles = state_tiles.at[:, :, :wave_count, :].add(-jnp.transpose(change, (1, 2, 0, 3)))
        b_strip = b_upper.reshape(blocks, TILE, W)[:wave_count]
        change = batch_product('jtu,juw->jtw', packed, b_strip).reshape(wave_count, TILE, blocks, TILE)
        keep_mask = tile_ids[None, :] > col_index[:, None]
        change = jnp.where(keep_mask[:, None, :, None], change, jnp.float32(0.0))
        state_tiles = state_tiles.at[offset:, :, :, :].add(-change)
    return state_tiles.reshape(W, W)
```

```python
import jax
import jax.numpy as jnp
from jax import lax
from jax.sharding import PartitionSpec as P

ROWS, COLS = 32, 16
GROUPS = ((2,), (1,), (0,))


def send(x, pairs):
    flat = [(a * COLS + b, c * COLS + d) for (a, b), (c, d) in pairs]
    return lax.ppermute(x, ("row", "col"), flat)


def band(offsets, rows, cols):
    pairs = []
    for c in range(COLS):
        for d in offsets:
            r = 2 * c + d
            if 0 <= r < ROWS and 0 <= r + rows < ROWS and 0 <= c + cols < COLS:
                pairs.append(((r, c), (r + rows, c + cols)))
    return pairs


def dot(a, b):
    return jnp.dot(a, b, preferred_element_type=jnp.float32)


def tile_solve(residue, left, right):
    left_vectors, left_inverse, left_values = left
    right_vectors, right_inverse, right_values = right
    first = dot(left_inverse, residue.astype(jnp.bfloat16)).astype(jnp.bfloat16)
    second = dot(first, right_vectors)
    divisor = left_values.astype(jnp.float32)[:, None] + right_values.astype(jnp.float32)[None, :]
    third = (second / divisor).astype(jnp.bfloat16)
    fourth = dot(left_vectors, third).astype(jnp.bfloat16)
    return dot(fourth, right_inverse)


def row_tree(x, offset):
    chips = offset // 2
    for step in (4, 2, 1):
        pairs = []
        for k in range(ROWS):
            for away in range(0, 8, 2 * step):
                c = k // 2 + 2 * away
                if c + 2 * step < COLS:
                    pairs.append(((k, c), (k, c + 2 * step)))
        got = send(x, pairs)
        takes = (offset % 2 == 0) & (chips % (2 * step) == step)
        x = jnp.where(takes, got, x)
    pairs = []
    for k in range(ROWS):
        for c in range(k // 2, COLS, 2):
            if (c ^ 1) > k // 2:
                pairs.append(((k, c), (k, c ^ 1)))
    got = send(x, pairs)
    return jnp.where(offset % 2 == 0, x, got)


def col_spread(x, row, col):
    tile = x.shape[1]
    plane, z = row // 8, row % 8
    relative = plane ^ (col // 4)
    half, quarter = tile // 2, tile // 4
    diagonal = [(k // 8, k % 8, k // 2) for k in range(ROWS)]
    got = send(x[:, half:], [((p * 8 + s, c), ((3 - p) * 8 + s, c)) for p, s, c in diagonal])
    part = jnp.where(relative == 0, x[:, :half], got)
    pairs = []
    for p, s, c in diagonal:
        pairs.append(((p * 8 + s, c), ((p ^ 1) * 8 + s, c)))
        pairs.append((((3 - p) * 8 + s, c), (((3 - p) ^ 1) * 8 + s, c)))
    got = send(part[:, quarter:], pairs)
    first = (relative == 0) | (relative == 3)
    part = jnp.where(first, part[:, :quarter], got)
    source = (col % 4) // 2
    base = 2 * (col % 4)
    pairs = [((q * 8 + s, c), (q * 8 + 7 - s, c)) for _, s, c in diagonal for q in range(4)]
    got = send(part, pairs)
    part = jnp.where((z // 2) * 2 == base, part, got)
    pairs = []
    for _, s, c in diagonal:
        for q in range(4):
            for t in (s, 7 - s):
                pairs.append(((q * 8 + t, c), (q * 8 + (t ^ 2), c)))
    got = send(part, pairs)
    holds = ((z // 2) * 2 == base) | (((7 - z) // 2) * 2 == base)
    part = jnp.where(holds, part, got)
    every = [(r, c) for r in range(ROWS) for c in range(COLS)]
    got = send(part, [((r, c), (r ^ 1, c)) for r, c in every])
    is_second = (z % 2) ^ ((z // 4) != source).astype(jnp.int32)
    both = jnp.stack([jnp.where(is_second == 0, part, got), jnp.where(is_second == 0, got, part)])
    got = send(both, [((r, c), (r ^ 8, c)) for r, c in every])
    both = jnp.concatenate([jnp.where(first, both, got), jnp.where(first, got, both)], axis=2)
    got = send(both, [((r, c), (r ^ 24, c)) for r, c in every])
    upper = relative <= 1
    return jnp.concatenate([jnp.where(upper, both, got), jnp.where(upper, got, both)], axis=2)


def shards(
    c_matrix, a_upper, b_upper, a_vectors, a_inverse, b_vectors, b_inverse, a_values, b_values
):
    tile = a_vectors.shape[1]
    row = lax.axis_index("row")
    col = lax.axis_index("col")
    d = row - 2 * col
    left = (a_vectors, a_inverse, a_values)

    def halves(x):
        return x[:, :tile], x[:, tile:]

    def pick(condition, pair):
        return jnp.where(condition, pair[0], pair[1])

    c_tiles = halves(c_matrix)
    own_right = (b_vectors, b_inverse, b_values)
    right_one = tuple(send(v, band((0, 1), 1, 0)) for v in own_right)
    right_two = tuple(send(v, band((1, 2), 1, 0)) for v in right_one)
    b_tiles = halves(b_upper)
    near = pick(d == -1, b_tiles)
    b_wave = send(near, band((-1, 0), 2, 0))
    b_one = send(near, band((-1, 0), 1, 0))
    b_two = send(pick(d == -2, b_tiles), band((-2, -1), 2, 0))
    a_next = lax.ppermute(a_upper, "col", [(c, c - 1) for c in range(1, COLS)])
    a_tiles, n_tiles = halves(a_upper), halves(a_next)
    above = [
        ((r, c), (r + 1, c)) for r in range(ROWS - 1) for c in range(COLS) if r + 1 <= 2 * c
    ]
    b_above = send(b_upper, above)
    b_above_two = send(b_above, above)

    solved_two = tile_solve(pick(d == 2, c_tiles), left, right_two)
    packed_two = solved_two.astype(jnp.bfloat16)
    below = send(packed_two, band((2, 3), -1, 0))
    col_two = send(packed_two, band((2, 3), -2, 0))
    row_two = send(packed_two, band((2, 3), 0, 1))

    residue = (
        pick(d == 1, c_tiles)
        - dot(pick(d == 1, n_tiles), below)
        - dot(jnp.where(d == 1, row_two, packed_two), b_wave)
    )
    solved_one = tile_solve(residue, left, right_one)
    packed_one = solved_one.astype(jnp.bfloat16)
    col_one = send(packed_one, band((1, 2), -1, 0))
    row_one = jnp.where(d == 1, packed_one, send(packed_one, band((2,), 0, 1)))

    residue = (
        pick(d == 0, c_tiles)
        - dot(pick(d == 0, n_tiles), col_two)
        - dot(row_two, b_two)
        - dot(jnp.where(d == 0, a_tiles[1], n_tiles[0]), col_one)
        - dot(row_one, b_one)
    )
    solved_zero = tile_solve(residue, left, own_right)
    packed_zero = solved_zero.astype(jnp.bfloat16)

    diagonal = (d == 0) | (d == 1)
    offset = col - row // 2
    a_all = (a_tiles[0], a_tiles[1], n_tiles[0], n_tiles[1])
    b_all = (b_upper, b_above, b_above_two)
    by_wave = {2: (col_two, row_two), 1: (col_one, row_one), 0: (packed_zero, packed_zero)}
    change = [0.0, 0.0]
    row_change = 0.0
    for group in GROUPS:
        down = col_spread(jnp.stack([by_wave[wave][0] for wave in group]), row, col)
        across = row_tree(jnp.stack([by_wave[wave][1] for wave in group]), offset)
        for index, wave in enumerate(group):
            for member in range(2):
                change[member] = change[member] + dot(a_all[member + wave], down[member, index])
            row_change = row_change + dot(across[index], b_all[wave])
    out = []
    for member, value in enumerate(halves(row_change)):
        where = d - member
        updated = c_tiles[member] - (change[member] + value)
        kept = jnp.where(where < 0, updated, c_tiles[member])
        kept = jnp.where(where == 0, solved_zero, kept)
        kept = jnp.where(where == 1, solved_one, kept)
        out.append(jnp.where(where == 2, solved_two, kept))
    return jnp.concatenate(out, axis=1)


def solution(mesh):
    placed = (
        P("row", "col"),
        P("row", "col"),
        P("row", "col"),
        P("row", None),
        P("row", None),
        P("row", None),
        P("row", None),
        P("row"),
        P("row"),
    )
    return jax.shard_map(
        shards, mesh=mesh, in_specs=placed, out_specs=P("row", "col"), check_vma=False
    )
```

```python
import jax
import jax.numpy as jnp
from jax import lax
from jax.experimental import pallas as pl
from jax.experimental.pallas import tpu as pltpu
from jax.sharding import PartitionSpec as P

ROWS, COLS = 32, 16


def send(x, pairs):
    flat = [(a * COLS + b, c * COLS + d) for (a, b), (c, d) in pairs]
    return lax.ppermute(x, ("row", "col"), flat)


def band(offsets, rows, cols):
    pairs = []
    for c in range(COLS):
        for d in offsets:
            r = 2 * c + d
            if 0 <= r < ROWS and 0 <= r + rows < ROWS and 0 <= c + cols < COLS:
                pairs.append(((r, c), (r + rows, c + cols)))
    return pairs


def dot(a, b):
    return jnp.dot(a, b, preferred_element_type=jnp.float32)


def solve(residue, left, right):
    left_vectors, left_inverse, left_values = left
    right_packed, right_inverse = right
    tile = residue.shape[0]
    first = dot(left_inverse[...], residue.astype(jnp.bfloat16)).astype(jnp.bfloat16)
    second = dot(first, right_packed[:tile, :])
    right_values = right_packed[tile:, :].astype(jnp.float32)[:1]
    third = (second / (left_values[...] + right_values)).astype(jnp.bfloat16)
    fourth = dot(left_vectors[...], third).astype(jnp.bfloat16)
    return dot(fourth, right_inverse[...])


def tile_of(ref, slot):
    tile = ref.shape[0]
    return ref[:, pl.ds(pl.multiple_of(slot * tile, tile), tile)]


def either(condition, first, second):
    chosen = jnp.where(condition, first.astype(jnp.float32), second.astype(jnp.float32))
    return chosen.astype(jnp.bfloat16)


def first_wave(info, c, u, p, lam, vm, q, x, xb):
    value = solve(tile_of(c, info[0]), (u, p, lam), (vm, q))
    x[...] = value
    xb[...] = value.astype(jnp.bfloat16)


def second_wave(info, c, n, below, across, own, b_band, u, p, lam, vm, q, x, xb):
    slot = info[1]
    left = either(slot == 0, across[...], own[...])
    residue = tile_of(c, slot) - dot(tile_of(n, slot), below[...]) - dot(left, tile_of(b_band, slot))
    value = solve(residue, (u, p, lam), (vm, q))
    x[...] = value
    xb[...] = value.astype(jnp.bfloat16)


def third_wave(
    info, c, a, n, col_two, row_two, col_one, row_one, own, b_band, b_above, u, p, lam, vm, q,
    x, down, across,
):
    slot = info[2]
    tile = x.shape[0]
    left = either(slot == 0, row_one[...], own[...])
    a_tile = either(slot == 0, a[:, tile:], n[:, :tile])
    residue = (
        tile_of(c, slot)
        - dot(tile_of(n, slot), col_two[...])
        - dot(row_two[...], tile_of(b_band, slot))
        - dot(a_tile, col_one[...])
        - dot(left, tile_of(b_above, slot))
    )
    value = solve(residue, (u, p, lam), (vm, q))
    x[...] = value
    packed = value.astype(jnp.bfloat16)
    down[0] = col_one[...]
    down[1] = packed
    across[0] = left
    across[1] = packed


def last_update(
    info, c, a, n, b, b_above, b_above_two, down_two, down, row_two, across, x_two, x_one, x_zero, out
):
    tile = c.shape[0]
    a_tiles = (a.at[:, :tile], a.at[:, tile:], n.at[:, :tile], n.at[:, tile:])
    for member in range(2):
        where = info[3] - member
        span = slice(member * tile, (member + 1) * tile)

        @pl.when(where < 0)
        def _():
            change = dot(a_tiles[member][...], down[member, 1])
            change += dot(a_tiles[member + 1][...], down[member, 0])
            change += dot(a_tiles[member + 2][...], down_two[member, 0])
            change += dot(across[1], b[:, span])
            change += dot(across[0], b_above[:, span])
            change += dot(row_two[0], b_above_two[:, span])
            out[:, span] = c[:, span] - change

        for wave, solved in enumerate((x_zero, x_one, x_two)):

            @pl.when(where == wave)
            def _():
                out[:, span] = solved[...]

        @pl.when(where > 2)
        def _():
            out[:, span] = c[:, span]


def run(kernel, outs, dots, info, *operands):
    tile = operands[0].shape[0]
    moved = sum(v.size * v.dtype.itemsize for v in (*operands, *outs))
    whole = pl.BlockSpec(memory_space=pltpu.VMEM)
    return pl.pallas_call(
        kernel,
        out_shape=outs,
        in_specs=[pl.BlockSpec(memory_space=pltpu.SMEM)] + [whole] * len(operands),
        out_specs=[whole] * len(outs),
        cost_estimate=pl.CostEstimate(
            flops=2 * dots * tile**3, bytes_accessed=moved, transcendentals=0
        ),
    )(info, *operands)


def row_tree(x, offset):
    chips = offset // 2
    for step in (4, 2, 1):
        pairs = []
        for k in range(ROWS):
            for away in range(0, 8, 2 * step):
                c = k // 2 + 2 * away
                if c + 2 * step < COLS:
                    pairs.append(((k, c), (k, c + 2 * step)))
        got = send(x, pairs)
        takes = (offset % 2 == 0) & (chips % (2 * step) == step)
        x = jnp.where(takes, got, x)
    pairs = []
    for k in range(ROWS):
        for c in range(k // 2, COLS, 2):
            if (c ^ 1) > k // 2:
                pairs.append(((k, c), (k, c ^ 1)))
    got = send(x, pairs)
    return jnp.where(offset % 2 == 0, x, got)


def col_spread(x, row, col):
    tile = x.shape[1]
    plane, z = row // 8, row % 8
    relative = plane ^ (col // 4)
    half, quarter = tile // 2, tile // 4
    diagonal = [(k // 8, k % 8, k // 2) for k in range(ROWS)]
    got = send(x[:, half:], [((p * 8 + s, c), ((3 - p) * 8 + s, c)) for p, s, c in diagonal])
    part = jnp.where(relative == 0, x[:, :half], got)
    pairs = []
    for p, s, c in diagonal:
        pairs.append(((p * 8 + s, c), ((p ^ 1) * 8 + s, c)))
        pairs.append((((3 - p) * 8 + s, c), (((3 - p) ^ 1) * 8 + s, c)))
    got = send(part[:, quarter:], pairs)
    first = (relative == 0) | (relative == 3)
    part = jnp.where(first, part[:, :quarter], got)
    source = (col % 4) // 2
    base = 2 * (col % 4)
    pairs = [((q * 8 + s, c), (q * 8 + 7 - s, c)) for _, s, c in diagonal for q in range(4)]
    got = send(part, pairs)
    part = jnp.where((z // 2) * 2 == base, part, got)
    pairs = []
    for _, s, c in diagonal:
        for q in range(4):
            for t in (s, 7 - s):
                pairs.append(((q * 8 + t, c), (q * 8 + (t ^ 2), c)))
    got = send(part, pairs)
    holds = ((z // 2) * 2 == base) | (((7 - z) // 2) * 2 == base)
    part = jnp.where(holds, part, got)
    every = [(r, c) for r in range(ROWS) for c in range(COLS)]
    got = send(part, [((r, c), (r ^ 1, c)) for r, c in every])
    is_second = (z % 2) ^ ((z // 4) != source).astype(jnp.int32)
    both = jnp.stack([jnp.where(is_second == 0, part, got), jnp.where(is_second == 0, got, part)])
    got = send(both, [((r, c), (r ^ 8, c)) for r, c in every])
    both = jnp.concatenate([jnp.where(first, both, got), jnp.where(first, got, both)], axis=2)
    got = send(both, [((r, c), (r ^ 24, c)) for r, c in every])
    upper = relative <= 1
    return jnp.concatenate([jnp.where(upper, both, got), jnp.where(upper, got, both)], axis=2)


def shards(
    c_matrix, a_upper, b_upper, a_vectors, a_inverse, b_vectors, b_inverse, a_values, b_values
):
    tile = a_vectors.shape[1]
    row = lax.axis_index("row")
    col = lax.axis_index("col")
    d = row - 2 * col
    info = jnp.stack([jnp.clip(d - 2, 0, 1), jnp.clip(d - 1, 0, 1), jnp.clip(d, 0, 1), d])
    left = (a_vectors, a_inverse, a_values.astype(jnp.float32)[:, None])
    square = jax.ShapeDtypeStruct((tile, tile), jnp.bfloat16)
    exact = jax.ShapeDtypeStruct((tile, tile), jnp.float32)
    pair = jax.ShapeDtypeStruct((2, tile, tile), jnp.bfloat16)

    packed = jnp.concatenate([b_vectors, jnp.broadcast_to(b_values[None], (16, tile))])
    packed_one = send(packed, band((0, 1), 1, 0))
    inverse_one = send(b_inverse, band((0, 1), 1, 0))
    packed_two = send(packed_one, band((1, 2), 1, 0))
    inverse_two = send(inverse_one, band((1, 2), 1, 0))
    b_band = send(b_upper, band((-2, -1, 0), 2, 0))
    a_next = send(a_upper, [((r, c), (r, c - 1)) for r in range(ROWS) for c in range(1, COLS)])

    def rows_down(last):
        rows = range(ROWS - 1)
        return [((r, c), (r + 1, c)) for r in rows for c in range(COLS) if r + 1 <= 2 * c + last]

    b_above = send(b_upper, rows_down(1))
    b_above_two = send(b_above, rows_down(0))

    x_two, solved_two = run(first_wave, (exact, square), 4, info, c_matrix, *left, packed_two, inverse_two)
    below = send(solved_two, band((2, 3), -1, 0))
    row_two = send(solved_two, band((2, 3), 0, 1))
    col_two = send(solved_two, band((2, 3), -2, 0))
    x_one, solved_one = run(
        second_wave, (exact, square), 6, info,
        c_matrix, a_next, below, row_two, solved_two, b_band, *left, packed_one, inverse_one,
    )
    col_one = send(solved_one, band((1, 2), -1, 0))
    row_one = send(solved_one, band((2,), 0, 1))
    x_zero, down, across = run(
        third_wave, (exact, pair, pair), 8, info,
        c_matrix, a_upper, a_next, col_two, row_two, col_one, row_one, solved_one,
        b_band, b_above, *left, packed, b_inverse,
    )
    offset = col - row // 2
    down_two = col_spread(col_two[None], row, col)
    across_two = row_tree(row_two[None], offset)
    down = col_spread(down, row, col)
    across = row_tree(across, offset)
    return run(
        last_update, (jax.ShapeDtypeStruct(c_matrix.shape, jnp.float32),), 12, info,
        c_matrix, a_upper, a_next, b_upper, b_above, b_above_two,
        down_two, down, across_two, across, x_two, x_one, x_zero,
    )[0]


def solution(mesh):
    placed = (
        P("row", "col"),
        P("row", "col"),
        P("row", "col"),
        P("row", None),
        P("row", None),
        P("row", None),
        P("row", None),
        P("row"),
        P("row"),
    )

    return jax.shard_map(shards, mesh=mesh, in_specs=placed, out_specs=P("row", "col"), check_vma=False)
```

```python
import jax
import jax.numpy as jnp
from jax import lax
from jax.experimental import pallas as pl
from jax.experimental.pallas import tpu as pltpu
from jax.sharding import PartitionSpec as P

ROWS, COLS = 32, 16
GRANT = {"K2": 12, "K1": 16, "K0": 20, "KF": 28}


def send(x, pairs):
    flat = [(a * COLS + b, c * COLS + d) for (a, b), (c, d) in pairs]
    return lax.ppermute(x, ("row", "col"), flat)


def band(offsets, rows, cols):
    pairs = []
    for c in range(COLS):
        for d in offsets:
            r = 2 * c + d
            if 0 <= r < ROWS and 0 <= r + rows < ROWS and 0 <= c + cols < COLS:
                pairs.append(((r, c), (r + rows, c + cols)))
    return pairs


def dot(a, b):
    return jnp.dot(a, b, preferred_element_type=jnp.float32)


def solve(residue, left, right):
    left_vectors, left_inverse, left_values = left
    right_packed, right_inverse = right
    tile = residue.shape[0]
    first = dot(left_inverse[...], residue.astype(jnp.bfloat16)).astype(jnp.bfloat16)
    second = dot(first, right_packed[:tile, :])
    right_values = right_packed[tile:, :].astype(jnp.float32)[:1]
    third = (second / (left_values[...] + right_values)).astype(jnp.bfloat16)
    fourth = dot(left_vectors[...], third).astype(jnp.bfloat16)
    return dot(fourth, right_inverse[...])


def tile_of(ref, slot):
    tile = ref.shape[0]
    return ref[:, pl.ds(pl.multiple_of(slot * tile, tile), tile)]


def either(condition, first, second):
    chosen = jnp.where(condition, first.astype(jnp.float32), second.astype(jnp.float32))
    return chosen.astype(jnp.bfloat16)


def first_wave(c, u, p, lam, vm, q, x, xb):
    value = solve(c[...], (u, p, lam), (vm, q))
    x[...] = value
    xb[...] = value.astype(jnp.bfloat16)


def second_wave(info, c, n, below, across, own, b_band, u, p, lam, vm, q, x, xb):
    slot = info[1]
    left = either(slot == 0, across[...], own[...])
    residue = c[...] - dot(tile_of(n, slot), below[...]) - dot(left, tile_of(b_band, slot))
    value = solve(residue, (u, p, lam), (vm, q))
    x[...] = value
    xb[...] = value.astype(jnp.bfloat16)


def third_wave(
    info, c, a, n, col_two, row_two, col_one, row_one, own, b_band, b_above, u, p, lam, vm, q,
    x, down, across,
):
    slot = info[2]
    tile = x.shape[0]
    left = either(slot == 0, row_one[...], own[...])
    a_tile = either(slot == 0, a[:, tile:], n[:, :tile])
    residue = (
        c[...]
        - dot(tile_of(n, slot), col_two[...])
        - dot(row_two[...], tile_of(b_band, slot))
        - dot(a_tile, col_one[...])
        - dot(left, tile_of(b_above, slot))
    )
    value = solve(residue, (u, p, lam), (vm, q))
    x[...] = value
    packed = value.astype(jnp.bfloat16)
    down[0] = packed
    down[1] = col_one[...]
    down[2] = col_two[...]
    across[0] = packed
    across[1] = left
    across[2] = row_two[...]


def last_update(
    info, c, a, n, b, b_above, b_above_two, p_one, p_two, q_one, q_two, across, flipped,
    x_two, x_one, x_zero, out, down,
):
    tile = c.shape[0]
    piece = p_one.shape[-2]
    a_tiles = (a.at[:, :tile], a.at[:, tile:], n.at[:, :tile], n.at[:, tile:])
    b_tiles = (b, b_above, b_above_two)
    where = info[3]

    @pl.when(where < 1)
    def _():
        for wave in range(3):
            for member in range(2):
                index = member ^ info[4]
                for start, (first, second) in ((0, (p_one, p_two)), (piece, (q_one, q_two))):
                    near = 5 if start == 0 else 9
                    for slot in range(2):
                        at = pl.ds(pl.multiple_of(info[near + slot] * 2 * piece + start, 16), piece)
                        down[member, wave, at, :] = first[slot, index, wave]
                        at = pl.ds(
                            pl.multiple_of(info[near + 2 + slot] * 2 * piece + start, 16), piece
                        )
                        down[member, wave, at, :] = second[slot, index, wave]

    def update(member, source):
        span = slice(member * tile, (member + 1) * tile)
        change = dot(a_tiles[member][...], down[member, 0])
        for wave in (1, 2):
            change += dot(a_tiles[member + wave][...], down[member, wave])
        for wave in range(3):
            change += dot(source[wave], b_tiles[wave][:, span])
        out[:, span] = c[:, span] - change

    for member in range(2):
        span = slice(member * tile, (member + 1) * tile)

        @pl.when((where < member) & (info[13] == 0))
        def _():
            update(member, across)

        @pl.when((where < member) & (info[13] == 1))
        def _():
            update(member, flipped)

        for wave, solved in enumerate((x_zero, x_one, x_two)):

            @pl.when(where == wave + member)
            def _():
                out[:, span] = solved[...]

        @pl.when(where > 2 + member)
        def _():
            out[:, span] = c[:, span]


def run(name, kernel, outs, dots, info, *operands, scratch=()):
    tile = operands[0].shape[0]
    moved = sum(v.size * v.dtype.itemsize for v in (*operands, *outs))
    whole = pl.BlockSpec(memory_space=pltpu.VMEM)
    scalars = () if info is None else (info,)
    return pl.pallas_call(
        kernel,
        out_shape=outs,
        in_specs=[pl.BlockSpec(memory_space=pltpu.SMEM)] * len(scalars) + [whole] * len(operands),
        out_specs=[whole] * len(outs),
        scratch_shapes=scratch,
        compiler_params=pltpu.CompilerParams(vmem_limit_bytes=GRANT[name] << 20),
        cost_estimate=pl.CostEstimate(
            flops=2 * dots * tile**3, bytes_accessed=moved, transcendentals=0
        ),
    )(*scalars, *operands)


def row_tree(x, offset):
    chips = offset // 2
    for step in (4, 2, 1):
        pairs = []
        for k in range(ROWS):
            for away in range(0, 8, 2 * step):
                c = k // 2 + 2 * away
                if c + 2 * step < COLS:
                    pairs.append(((k, c), (k, c + 2 * step)))
        got = send(x, pairs)
        takes = (offset % 2 == 0) & (chips % (2 * step) == step)
        x = jnp.where(takes, got, x)
    pairs = []
    for k in range(ROWS):
        for c in range(k // 2, COLS, 2):
            if (c ^ 1) > k // 2:
                pairs.append(((k, c), (k, c ^ 1)))
    got = send(x, pairs)
    return x, got


def col_spread(x, row, col):
    tile = x.shape[1]
    plane, z = row // 8, row % 8
    relative = plane ^ (col // 4)
    half, quarter = tile // 2, tile // 4
    diagonal = [(k // 8, k % 8, k // 2) for k in range(ROWS)]
    got = send(x[:, half:], [((p * 8 + s, c), ((3 - p) * 8 + s, c)) for p, s, c in diagonal])
    part = jnp.where(relative == 0, x[:, :half], got)
    pairs = []
    for p, s, c in diagonal:
        pairs.append(((p * 8 + s, c), ((p ^ 1) * 8 + s, c)))
        pairs.append((((3 - p) * 8 + s, c), (((3 - p) ^ 1) * 8 + s, c)))
    got = send(part[:, quarter:], pairs)
    first = (relative == 0) | (relative == 3)
    part = jnp.where(first, part[:, :quarter], got)
    base = 2 * (col % 4)
    pairs = [((q * 8 + s, c), (q * 8 + 7 - s, c)) for _, s, c in diagonal for q in range(4)]
    got = send(part, pairs)
    part = jnp.where((z // 2) * 2 == base, part, got)
    pairs = []
    for _, s, c in diagonal:
        for q in range(4):
            for t in (s, 7 - s):
                pairs.append(((q * 8 + t, c), (q * 8 + (t ^ 2), c)))
    got = send(part, pairs)
    holds = ((z // 2) * 2 == base) | (((7 - z) // 2) * 2 == base)
    part = jnp.where(holds, part, got)
    every = [(r, c) for r in range(ROWS) for c in range(COLS)]
    got = send(part, [((r, c), (r ^ 1, c)) for r, c in every])
    both = jnp.stack([part, got])
    near = [((r, c), (r ^ 8, c)) for r, c in every]
    far = [((r, c), (r ^ 24, c)) for r, c in every]
    piece = tile // 8
    p_one = both[:, :, :piece]
    q_one = both[:, :, piece:]
    p_one = jnp.stack([p_one, send(p_one, near)])
    q_one = jnp.stack([q_one, send(q_one, far)])
    return p_one, send(p_one, far), q_one, send(q_one, near)


def shards(
    c_matrix, a_upper, b_upper, a_vectors, a_inverse, b_vectors, b_inverse, a_values, b_values
):
    tile = a_vectors.shape[1]
    row = lax.axis_index("row")
    col = lax.axis_index("col")
    d = row - 2 * col
    relative = (row // 8) ^ (col // 4)
    z = row % 8
    flips = [relative ^ flip for flip in (0, 1, 3, 2, 0, 3, 1, 2)]
    order = [plane ^ (plane // 2) for plane in flips]
    swapped = (z % 2) ^ ((z // 4) != (col % 4) // 2).astype(jnp.int32)
    parity = jnp.abs(col - row // 2) % 2
    slots = [jnp.clip(d - wave, 0, 1) for wave in (2, 1, 0)]
    info = jnp.stack([*slots, d, swapped, *order, parity])
    c_two, c_one, c_zero = (
        lax.dynamic_slice_in_dim(c_matrix, slot * a_vectors.shape[1], a_vectors.shape[1], 1)
        for slot in slots
    )
    left = (a_vectors, a_inverse, a_values.astype(jnp.float32)[:, None])
    square = jax.ShapeDtypeStruct((tile, tile), jnp.bfloat16)
    exact = jax.ShapeDtypeStruct((tile, tile), jnp.float32)
    three = jax.ShapeDtypeStruct((3, tile, tile), jnp.bfloat16)

    packed = jnp.concatenate([b_vectors, jnp.broadcast_to(b_values[None], (16, tile))])
    packed_one = send(packed, band((0, 1), 1, 0))
    inverse_one = send(b_inverse, band((0, 1), 1, 0))
    packed_two = send(packed_one, band((1, 2), 1, 0))
    inverse_two = send(inverse_one, band((1, 2), 1, 0))
    b_band = send(b_upper, band((-2, -1, 0), 2, 0))
    a_next = send(a_upper, [((r, c), (r, c - 1)) for r in range(ROWS) for c in range(1, COLS)])

    def rows_down(last):
        rows = range(ROWS - 1)
        return [((r, c), (r + 1, c)) for r in rows for c in range(COLS) if r + 1 <= 2 * c + last]

    b_above = send(b_upper, rows_down(1))
    b_above_two = send(b_above, rows_down(0))

    x_two, solved_two = run(
        "K2", first_wave, (exact, square), 4, None,
        c_two.astype(jnp.bfloat16), *left, packed_two, inverse_two,
    )
    below = send(solved_two, band((2, 3), -1, 0))
    row_two = send(solved_two, band((2, 3), 0, 1))
    col_two = send(solved_two, band((2, 3), -2, 0))
    x_one, solved_one = run(
        "K1", second_wave, (exact, square), 6, info,
        c_one, a_next, below, row_two, solved_two, b_band, *left, packed_one, inverse_one,
    )
    col_one = send(solved_one, band((1, 2), -1, 0))
    row_one = send(solved_one, band((2,), 0, 1))
    x_zero, down, across = run(
        "K0", third_wave, (exact, three, three), 8, info,
        c_zero, a_upper, a_next, col_two, row_two, col_one, row_one, solved_one,
        b_band, b_above, *left, packed, b_inverse,
    )
    offset = col - row // 2
    pieces = col_spread(down, row, col)
    across, flipped = row_tree(across, offset)
    return run(
        "KF", last_update, (jax.ShapeDtypeStruct(c_matrix.shape, jnp.float32),), 12, info,
        c_matrix, a_upper, a_next, b_upper, b_above, b_above_two,
        *pieces, across, flipped, x_two, x_one, x_zero,
        scratch=[pltpu.VMEM((2, 3, tile, tile), jnp.bfloat16)],
    )[0]


def solution(mesh):
    placed = (
        P("row", "col"),
        P("row", "col"),
        P("row", "col"),
        P("row", None),
        P("row", None),
        P("row", None),
        P("row", None),
        P("row"),
        P("row"),
    )

    return jax.shard_map(
        shards, mesh=mesh, in_specs=placed, out_specs=P("row", "col"), check_vma=False
    )
```

```python
import jax
import jax.numpy as jnp
from jax import lax
from jax.experimental import pallas as pl
from jax.experimental.pallas import tpu as pltpu
from jax.sharding import PartitionSpec as P

ROWS, COLS = 32, 16
GRANT = {"K2": 12, "K1": 16, "K0": 20, "KF": 28}


def send(x, pairs):
    flat = [(a * COLS + b, c * COLS + d) for (a, b), (c, d) in pairs]
    return lax.ppermute(x, ("row", "col"), flat)


def band(offsets, rows, cols):
    pairs = []
    for c in range(COLS):
        for d in offsets:
            r = 2 * c + d
            if 0 <= r < ROWS and 0 <= r + rows < ROWS and 0 <= c + cols < COLS:
                pairs.append(((r, c), (r + rows, c + cols)))
    return pairs


def dot(a, b):
    return jnp.dot(a, b, preferred_element_type=jnp.float32)


def solve(residue, left, right):
    left_vectors, left_inverse, left_values = left
    right_vectors, right_inverse, right_values = right
    first = dot(left_inverse[...], residue.astype(jnp.bfloat16)).astype(jnp.bfloat16)
    second = dot(first, right_vectors[...])
    third = (second / (left_values[...] + right_values[...])).astype(jnp.bfloat16)
    fourth = dot(left_vectors[...], third).astype(jnp.bfloat16)
    return dot(fourth, right_inverse[...])


def tile_of(ref, slot):
    tile = ref.shape[0]
    return ref[:, pl.ds(pl.multiple_of(slot * tile, tile), tile)]


def either(condition, first, second):
    chosen = jnp.where(condition, first.astype(jnp.float32), second.astype(jnp.float32))
    return chosen.astype(jnp.bfloat16)


def first_wave(c, u, p, lam, v, q, mu, x, xb):
    value = solve(c[...], (u, p, lam), (v, q, mu))
    x[...] = value
    xb[...] = value.astype(jnp.bfloat16)


def second_wave(info, c, n, below, across, own, b_band, u, p, lam, v, q, mu, x, xb):
    slot = info[1]
    left = either(slot == 0, across[...], own[...])
    residue = c[...] - dot(tile_of(n, slot), below[...]) - dot(left, tile_of(b_band, slot))
    value = solve(residue, (u, p, lam), (v, q, mu))
    x[...] = value
    xb[...] = value.astype(jnp.bfloat16)


def third_wave(
    info, c, a, n, col_two, row_two, col_one, row_one, own, b_band, b_above, u, p, lam, v, q, mu,
    x, *parts,
):
    slot = info[2]
    tile = x.shape[0]
    left = either(slot == 0, row_one[...], own[...])
    a_tile = either(slot == 0, a[:, tile:], n[:, :tile])
    residue = (
        c[...]
        - dot(tile_of(n, slot), col_two[...])
        - dot(row_two[...], tile_of(b_band, slot))
        - dot(a_tile, col_one[...])
        - dot(left, tile_of(b_above, slot))
    )
    value = solve(residue, (u, p, lam), (v, q, mu))
    x[...] = value
    packed = value.astype(jnp.bfloat16)
    across = parts[-1]
    quarter = tile // 4
    for index in range(4):
        rows = slice(index * quarter, (index + 1) * quarter)
        parts[index][0] = packed[rows]
        parts[index][1] = col_one[rows, :]
        parts[index][2] = col_two[rows, :]
    across[0] = packed
    across[1] = left
    across[2] = row_two[...]


def last_update(
    info, c, a, n, b, b_above, b_above_two, p_one, p_two, q_one, q_two, across, flipped,
    x_two, x_one, x_zero, out, down,
):
    tile = c.shape[0]
    piece = p_one.shape[-2]
    a_tiles = (a.at[:, :tile], a.at[:, tile:], n.at[:, :tile], n.at[:, tile:])
    b_tiles = (b, b_above, b_above_two)
    where = info[3]

    @pl.when(where < 1)
    def _():
        for wave in range(3):
            for member in range(2):
                index = member ^ info[4]
                for start, (first, second) in ((0, (p_one, p_two)), (piece, (q_one, q_two))):
                    near = 5 if start == 0 else 9
                    for slot in range(2):
                        at = pl.ds(pl.multiple_of(info[near + slot] * 2 * piece + start, 16), piece)
                        down[member, wave, at, :] = first[slot, index, wave]
                        at = pl.ds(
                            pl.multiple_of(info[near + 2 + slot] * 2 * piece + start, 16), piece
                        )
                        down[member, wave, at, :] = second[slot, index, wave]

    def update(member, source):
        span = slice(member * tile, (member + 1) * tile)
        change = dot(a_tiles[member][...], down[member, 0])
        for wave in (1, 2):
            change += dot(a_tiles[member + wave][...], down[member, wave])
        for wave in range(3):
            change += dot(source[wave], b_tiles[wave][:, span])
        out[:, span] = c[:, span] - change

    for member in range(2):
        span = slice(member * tile, (member + 1) * tile)

        @pl.when((where < member) & (info[13] == 0))
        def _():
            update(member, across)

        @pl.when((where < member) & (info[13] == 1))
        def _():
            update(member, flipped)

        for wave, solved in enumerate((x_zero, x_one, x_two)):

            @pl.when(where == wave + member)
            def _():
                out[:, span] = solved[...]

        @pl.when(where > 2 + member)
        def _():
            out[:, span] = c[:, span]


def run(name, kernel, outs, dots, info, *operands, scratch=()):
    tile = operands[0].shape[0]
    moved = sum(v.size * v.dtype.itemsize for v in (*operands, *outs))
    whole = pl.BlockSpec(memory_space=pltpu.VMEM)
    scalars = () if info is None else (info,)
    return pl.pallas_call(
        kernel,
        out_shape=outs,
        in_specs=[pl.BlockSpec(memory_space=pltpu.SMEM)] * len(scalars) + [whole] * len(operands),
        out_specs=[whole] * len(outs),
        scratch_shapes=scratch,
        compiler_params=pltpu.CompilerParams(vmem_limit_bytes=GRANT[name] << 20),
        cost_estimate=pl.CostEstimate(
            flops=2 * dots * tile**3, bytes_accessed=moved, transcendentals=0
        ),
    )(*scalars, *operands)


def row_tree(x, offset):
    chips = offset // 2
    for step in (4, 2, 1):
        pairs = []
        for k in range(ROWS):
            for away in range(0, 8, 2 * step):
                c = k // 2 + 2 * away
                if c + 2 * step < COLS:
                    pairs.append(((k, c), (k, c + 2 * step)))
        got = send(x, pairs)
        takes = (offset % 2 == 0) & (chips % (2 * step) == step)
        x = jnp.where(takes, got, x)
    pairs = []
    for k in range(ROWS):
        for c in range(k // 2, COLS, 2):
            if (c ^ 1) > k // 2:
                pairs.append(((k, c), (k, c ^ 1)))
    got = send(x, pairs)
    return x, got


def col_spread(quarters, row, col):
    z = row % 8
    relative = (row // 8) ^ (col // 4)
    diagonal = [(k // 8, k % 8, k // 2) for k in range(ROWS)]
    got = []
    for index, flip in ((1, 1), (2, 3), (3, 2)):
        pairs = [((p * 8 + s, c), ((p ^ flip) * 8 + s, c)) for p, s, c in diagonal]
        got.append(send(quarters[index], pairs))
    part = jnp.where(
        relative == 0,
        quarters[0],
        jnp.where(relative == 1, got[0], jnp.where(relative == 3, got[1], got[2])),
    )
    base = 2 * (col % 4)
    pairs = [((q * 8 + s, c), (q * 8 + 7 - s, c)) for _, s, c in diagonal for q in range(4)]
    got = send(part, pairs)
    part = jnp.where((z // 2) * 2 == base, part, got)
    pairs = []
    for _, s, c in diagonal:
        for q in range(4):
            for t in (s, 7 - s):
                pairs.append(((q * 8 + t, c), (q * 8 + (t ^ 2), c)))
    got = send(part, pairs)
    holds = ((z // 2) * 2 == base) | (((7 - z) // 2) * 2 == base)
    part = jnp.where(holds, part, got)
    every = [(r, c) for r in range(ROWS) for c in range(COLS)]
    got = send(part, [((r, c), (r ^ 1, c)) for r, c in every])
    both = jnp.stack([part, got])
    near = [((r, c), (r ^ 8, c)) for r, c in every]
    far = [((r, c), (r ^ 24, c)) for r, c in every]
    piece = part.shape[1] // 2
    p_one = both[:, :, :piece]
    q_one = both[:, :, piece:]
    p_one = jnp.stack([p_one, send(p_one, near)])
    q_one = jnp.stack([q_one, send(q_one, far)])
    return p_one, send(p_one, far), q_one, send(q_one, near)


def shards(
    c_matrix, a_upper, b_upper, a_vectors, a_inverse, b_vectors, b_inverse, a_values, b_values
):
    tile = a_vectors.shape[1]
    row = lax.axis_index("row")
    col = lax.axis_index("col")
    d = row - 2 * col
    relative = (row // 8) ^ (col // 4)
    z = row % 8
    flips = [relative ^ flip for flip in (0, 1, 3, 2, 0, 3, 1, 2)]
    order = [plane ^ (plane // 2) for plane in flips]
    swapped = (z % 2) ^ ((z // 4) != (col % 4) // 2).astype(jnp.int32)
    parity = jnp.abs(col - row // 2) % 2
    slots = [jnp.clip(d - wave, 0, 1) for wave in (2, 1, 0)]
    info = jnp.stack([*slots, d, swapped, *order, parity])
    c_two, c_one, c_zero = (
        lax.dynamic_slice_in_dim(c_matrix, slot * a_vectors.shape[1], a_vectors.shape[1], 1)
        for slot in slots
    )
    left = (a_vectors, a_inverse, a_values.astype(jnp.float32)[:, None])
    square = jax.ShapeDtypeStruct((tile, tile), jnp.bfloat16)
    exact = jax.ShapeDtypeStruct((tile, tile), jnp.float32)
    strip = jax.ShapeDtypeStruct((3, tile // 4, tile), jnp.bfloat16)
    three = jax.ShapeDtypeStruct((3, tile, tile), jnp.bfloat16)

    vectors_one = send(b_vectors, band((0, 1), 1, 0))
    inverse_one = send(b_inverse, band((0, 1), 1, 0))
    values_one = send(b_values, band((0, 1), 1, 0))
    vectors_two = send(vectors_one, band((1, 2), 1, 0))
    inverse_two = send(inverse_one, band((1, 2), 1, 0))
    values_two = send(values_one, band((1, 2), 1, 0))
    rights = [
        (vectors, inverse, values.astype(jnp.float32)[None])
        for vectors, inverse, values in (
            (b_vectors, b_inverse, b_values),
            (vectors_one, inverse_one, values_one),
            (vectors_two, inverse_two, values_two),
        )
    ]
    b_band = send(b_upper, band((-2, -1, 0), 2, 0))
    a_next = send(a_upper, [((r, c), (r, c - 1)) for r in range(ROWS) for c in range(1, COLS)])

    def rows_down(last):
        rows = range(ROWS - 1)
        return [((r, c), (r + 1, c)) for r in rows for c in range(COLS) if r + 1 <= 2 * c + last]

    b_above = send(b_upper, rows_down(1))
    b_above_two = send(b_above, rows_down(0))

    x_two, solved_two = run(
        "K2", first_wave, (exact, square), 4, None,
        c_two.astype(jnp.bfloat16), *left, *rights[2],
    )
    below = send(solved_two, band((2, 3), -1, 0))
    row_two = send(solved_two, band((2, 3), 0, 1))
    col_two = send(solved_two, band((2, 3), -2, 0))
    x_one, solved_one = run(
        "K1", second_wave, (exact, square), 6, info,
        c_one, a_next, below, row_two, solved_two, b_band, *left, *rights[1],
    )
    col_one = send(solved_one, band((1, 2), -1, 0))
    row_one = send(solved_one, band((2,), 0, 1))
    x_zero, *quarters, across = run(
        "K0", third_wave, (exact, *[strip] * 4, three), 8, info,
        c_zero, a_upper, a_next, col_two, row_two, col_one, row_one, solved_one,
        b_band, b_above, *left, *rights[0],
    )
    offset = col - row // 2
    pieces = col_spread(quarters, row, col)
    across, flipped = row_tree(across, offset)
    return run(
        "KF", last_update, (jax.ShapeDtypeStruct(c_matrix.shape, jnp.float32),), 12, info,
        c_matrix, a_upper, a_next, b_upper, b_above, b_above_two,
        *pieces, across, flipped, x_two, x_one, x_zero,
        scratch=[pltpu.VMEM((2, 3, tile, tile), jnp.bfloat16)],
    )[0]


def solution(mesh):
    placed = (
        P("row", "col"),
        P("row", "col"),
        P("row", "col"),
        P("row", None),
        P("row", None),
        P("row", None),
        P("row", None),
        P("row"),
        P("row"),
    )

    return jax.shard_map(
        shards, mesh=mesh, in_specs=placed, out_specs=P("row", "col"), check_vma=False
    )
```

```python
import jax
import jax.numpy as jnp
from jax import lax
from jax.experimental import pallas as pl
from jax.experimental.pallas import tpu as pltpu
from jax.sharding import PartitionSpec as P

ROWS, COLS = 32, 16
GRANT = {"K2": 12, "K1": 16, "K0": 20, "KF": 28}


def send(x, pairs):
    flat = [(a * COLS + b, c * COLS + d) for (a, b), (c, d) in pairs]
    return lax.ppermute(x, ("row", "col"), flat)


def band(offsets, rows, cols):
    pairs = []
    for c in range(COLS):
        for d in offsets:
            r = 2 * c + d
            if 0 <= r < ROWS and 0 <= r + rows < ROWS and 0 <= c + cols < COLS:
                pairs.append(((r, c), (r + rows, c + cols)))
    return pairs


def dot(a, b):
    return jnp.dot(a, b, preferred_element_type=jnp.float32)


def solve(residue, left, right):
    left_vectors, left_inverse, left_values = left
    right_vectors, right_inverse, right_values = right
    first = dot(left_inverse[...], residue.astype(jnp.bfloat16)).astype(jnp.bfloat16)
    second = dot(first, right_vectors[...])
    third = (second / (left_values[...] + right_values[...])).astype(jnp.bfloat16)
    fourth = dot(left_vectors[...], third).astype(jnp.bfloat16)
    return dot(fourth, right_inverse[...])


def tile_of(ref, slot):
    tile = ref.shape[0]
    return ref[:, pl.ds(pl.multiple_of(slot * tile, tile), tile)]


def either(condition, first, second):
    chosen = jnp.where(condition, first.astype(jnp.float32), second.astype(jnp.float32))
    return chosen.astype(jnp.bfloat16)


def first_wave(c, u, p, lam, v, q, mu, x, xb):
    value = solve(c[...], (u, p, lam), (v, q, mu))
    x[...] = value
    xb[...] = value.astype(jnp.bfloat16)


def second_wave(info, c, n, below, across, own, b_wave, u, p, lam, v, q, mu, x, xb):
    slot = info[1]
    left = either(slot == 0, across[...], own[...])
    residue = c[...] - dot(tile_of(n, slot), below[...]) - dot(left, b_wave[...])
    value = solve(residue, (u, p, lam), (v, q, mu))
    x[...] = value
    xb[...] = value.astype(jnp.bfloat16)


def third_wave(
    info, c, a, n, col_two, row_two, col_one, row_one, own, b_two, b_above, u, p, lam, v, q, mu,
    x, *parts,
):
    slot = info[2]
    tile = x.shape[0]
    left = either(slot == 0, row_one[...], own[...])
    a_tile = either(slot == 0, a[:, tile:], n[:, :tile])
    residue = (
        c[...]
        - dot(tile_of(n, slot), col_two[...])
        - dot(row_two[...], b_two[...])
        - dot(a_tile, col_one[...])
        - dot(left, tile_of(b_above, slot))
    )
    value = solve(residue, (u, p, lam), (v, q, mu))
    x[...] = value
    packed = value.astype(jnp.bfloat16)
    across = parts[-1]
    quarter = tile // 4
    for index in range(4):
        rows = slice(index * quarter, (index + 1) * quarter)
        parts[index][0] = packed[rows]
        parts[index][1] = col_one[rows, :]
        parts[index][2] = col_two[rows, :]
    across[0] = packed
    across[1] = left


def last_update(
    info, c, a, n, b, b_above, b_above_two, p_one, p_two, q_one, q_two, across, flipped,
    early, early_flipped,
    x_two, x_one, x_zero, out, down,
):
    tile = c.shape[0]
    piece = p_one.shape[-2]
    a_tiles = (a.at[:, :tile], a.at[:, tile:], n.at[:, :tile], n.at[:, tile:])
    b_tiles = (b, b_above, b_above_two)
    where = info[3]

    @pl.when(where < 1)
    def _():
        for wave in range(3):
            for member in range(2):
                index = member ^ info[4]
                for start, (first, second) in ((0, (p_one, p_two)), (piece, (q_one, q_two))):
                    near = 5 if start == 0 else 9
                    for slot in range(2):
                        at = pl.ds(pl.multiple_of(info[near + slot] * 2 * piece + start, 16), piece)
                        down[member, wave, at, :] = first[slot, index, wave]
                        at = pl.ds(
                            pl.multiple_of(info[near + 2 + slot] * 2 * piece + start, 16), piece
                        )
                        down[member, wave, at, :] = second[slot, index, wave]

    def update(member, source, source_two):
        span = slice(member * tile, (member + 1) * tile)
        change = dot(a_tiles[member][...], down[member, 0])
        for wave in (1, 2):
            change += dot(a_tiles[member + wave][...], down[member, wave])
        for wave in range(2):
            change += dot(source[wave], b_tiles[wave][:, span])
        change += dot(source_two[0], b_tiles[2][:, span])
        out[:, span] = c[:, span] - change

    for member in range(2):
        span = slice(member * tile, (member + 1) * tile)

        @pl.when((where < member) & (info[13] == 0))
        def _():
            update(member, across, early)

        @pl.when((where < member) & (info[13] == 1))
        def _():
            update(member, flipped, early_flipped)

        for wave, solved in enumerate((x_zero, x_one, x_two)):

            @pl.when(where == wave + member)
            def _():
                out[:, span] = solved[...]

        @pl.when(where > 2 + member)
        def _():
            out[:, span] = c[:, span]


def run(name, kernel, outs, dots, info, *operands, scratch=()):
    tile = operands[0].shape[0]
    moved = sum(v.size * v.dtype.itemsize for v in (*operands, *outs))
    whole = pl.BlockSpec(memory_space=pltpu.VMEM)
    scalars = () if info is None else (info,)
    return pl.pallas_call(
        kernel,
        out_shape=outs,
        in_specs=[pl.BlockSpec(memory_space=pltpu.SMEM)] * len(scalars) + [whole] * len(operands),
        out_specs=[whole] * len(outs),
        scratch_shapes=scratch,
        compiler_params=pltpu.CompilerParams(vmem_limit_bytes=GRANT[name] << 20),
        cost_estimate=pl.CostEstimate(
            flops=2 * dots * tile**3, bytes_accessed=moved, transcendentals=0
        ),
    )(*scalars, *operands)


def row_tree(x, offset):
    chips = offset // 2
    for step in (4, 2, 1):
        pairs = []
        for k in range(ROWS):
            for away in range(0, 8, 2 * step):
                c = k // 2 + 2 * away
                if c + 2 * step < COLS:
                    pairs.append(((k, c), (k, c + 2 * step)))
        got = send(x, pairs)
        takes = (offset % 2 == 0) & (chips % (2 * step) == step)
        x = jnp.where(takes, got, x)
    pairs = []
    for k in range(ROWS):
        for c in range(k // 2, COLS, 2):
            if (c ^ 1) > k // 2:
                pairs.append(((k, c), (k, c ^ 1)))
    got = send(x, pairs)
    return x, got


def col_spread(quarters, row, col):
    z = row % 8
    relative = (row // 8) ^ (col // 4)
    diagonal = [(k // 8, k % 8, k // 2) for k in range(ROWS)]
    got = []
    for index, flip in ((1, 1), (2, 3), (3, 2)):
        pairs = [((p * 8 + s, c), ((p ^ flip) * 8 + s, c)) for p, s, c in diagonal]
        got.append(send(quarters[index], pairs))
    part = jnp.where(
        relative == 0,
        quarters[0],
        jnp.where(relative == 1, got[0], jnp.where(relative == 3, got[1], got[2])),
    )
    base = 2 * (col % 4)
    pairs = [((q * 8 + s, c), (q * 8 + 7 - s, c)) for _, s, c in diagonal for q in range(4)]
    got = send(part, pairs)
    part = jnp.where((z // 2) * 2 == base, part, got)
    pairs = []
    for _, s, c in diagonal:
        for q in range(4):
            for t in (s, 7 - s):
                pairs.append(((q * 8 + t, c), (q * 8 + (t ^ 2), c)))
    got = send(part, pairs)
    holds = ((z // 2) * 2 == base) | (((7 - z) // 2) * 2 == base)
    part = jnp.where(holds, part, got)
    every = [(r, c) for r in range(ROWS) for c in range(COLS)]
    got = send(part, [((r, c), (r ^ 1, c)) for r, c in every])
    both = jnp.stack([part, got])
    near = [((r, c), (r ^ 8, c)) for r, c in every]
    far = [((r, c), (r ^ 24, c)) for r, c in every]
    piece = part.shape[1] // 2
    p_one = both[:, :, :piece]
    q_one = both[:, :, piece:]
    p_one = jnp.stack([p_one, send(p_one, near)])
    q_one = jnp.stack([q_one, send(q_one, far)])
    return p_one, send(p_one, far), q_one, send(q_one, near)


def shards(
    c_matrix, a_upper, b_upper, a_vectors, a_inverse, b_vectors, b_inverse, a_values, b_values
):
    tile = a_vectors.shape[1]
    row = lax.axis_index("row")
    col = lax.axis_index("col")
    d = row - 2 * col
    relative = (row // 8) ^ (col // 4)
    z = row % 8
    flips = [relative ^ flip for flip in (0, 1, 3, 2, 0, 3, 1, 2)]
    order = [plane ^ (plane // 2) for plane in flips]
    swapped = (z % 2) ^ ((z // 4) != (col % 4) // 2).astype(jnp.int32)
    parity = jnp.abs(col - row // 2) % 2
    slots = [jnp.clip(d - wave, 0, 1) for wave in (2, 1, 0)]
    info = jnp.stack([*slots, d, swapped, *order, parity])
    c_two, c_one, c_zero = (
        lax.dynamic_slice_in_dim(c_matrix, slot * a_vectors.shape[1], a_vectors.shape[1], 1)
        for slot in slots
    )
    left = (a_vectors, a_inverse, a_values.astype(jnp.float32)[:, None])
    square = jax.ShapeDtypeStruct((tile, tile), jnp.bfloat16)
    exact = jax.ShapeDtypeStruct((tile, tile), jnp.float32)
    strip = jax.ShapeDtypeStruct((3, tile // 4, tile), jnp.bfloat16)
    pair = jax.ShapeDtypeStruct((2, tile, tile), jnp.bfloat16)

    vectors_one = send(b_vectors, band((0, 1), 1, 0))
    inverse_one = send(b_inverse, band((0, 1), 1, 0))
    values_one = send(b_values, band((0, 1), 1, 0))
    vectors_two = send(vectors_one, band((1, 2), 1, 0))
    inverse_two = send(inverse_one, band((1, 2), 1, 0))
    values_two = send(values_one, band((1, 2), 1, 0))
    rights = [
        (vectors, inverse, values.astype(jnp.float32)[None])
        for vectors, inverse, values in (
            (b_vectors, b_inverse, b_values),
            (vectors_one, inverse_one, values_one),
            (vectors_two, inverse_two, values_two),
        )
    ]
    b_tiles = b_upper[:, :tile], b_upper[:, tile:]
    b_wave = send(jnp.where(d == -1, *b_tiles), band((-1, 0), 2, 0))
    b_two = send(jnp.where(d == -2, *b_tiles), band((-2, -1), 2, 0))
    a_next = send(a_upper, [((r, c), (r, c - 1)) for r in range(ROWS) for c in range(1, COLS)])

    def rows_down(last):
        rows = range(ROWS - 1)
        return [((r, c), (r + 1, c)) for r in rows for c in range(COLS) if r + 1 <= 2 * c + last]

    b_above = send(b_upper, rows_down(1))
    b_above_two = send(b_above, rows_down(0))

    x_two, solved_two = run(
        "K2", first_wave, (exact, square), 4, None,
        c_two.astype(jnp.bfloat16), *left, *rights[2],
    )
    below = send(solved_two, band((2, 3), -1, 0))
    row_two = send(solved_two, band((2, 3), 0, 1))
    col_two = send(solved_two, band((2, 3), -2, 0))
    offset = col - row // 2
    early, early_flipped = row_tree(row_two[None], offset)
    x_one, solved_one = run(
        "K1", second_wave, (exact, square), 6, info,
        c_one, a_next, below, row_two, solved_two, b_wave, *left, *rights[1],
    )
    col_one = send(solved_one, band((1, 2), -1, 0))
    row_one = send(solved_one, band((2,), 0, 1))
    x_zero, *quarters, across = run(
        "K0", third_wave, (exact, *[strip] * 4, pair), 8, info,
        c_zero, a_upper, a_next, col_two, row_two, col_one, row_one, solved_one,
        b_two, b_above, *left, *rights[0],
    )
    pieces = col_spread(quarters, row, col)
    across, flipped = row_tree(across, offset)
    return run(
        "KF", last_update, (jax.ShapeDtypeStruct(c_matrix.shape, jnp.float32),), 12, info,
        c_matrix, a_upper, a_next, b_upper, b_above, b_above_two,
        *pieces, across, flipped, early, early_flipped, x_two, x_one, x_zero,
        scratch=[pltpu.VMEM((2, 3, tile, tile), jnp.bfloat16)],
    )[0]


def solution(mesh):
    placed = (
        P("row", "col"),
        P("row", "col"),
        P("row", "col"),
        P("row", None),
        P("row", None),
        P("row", None),
        P("row", None),
        P("row"),
        P("row"),
    )

    return jax.shard_map(
        shards, mesh=mesh, in_specs=placed, out_specs=P("row", "col"), check_vma=False
    )
```

```python
import jax
import jax.numpy as jnp
from jax import lax
from jax.experimental import pallas as pl
from jax.experimental.pallas import tpu as pltpu
from jax.sharding import PartitionSpec as P

ROWS, COLS = 32, 16
GRANT = {"K2": 12, "K1": 16, "K0": 20, "KF": 28}


def send(x, pairs):
    flat = [(a * COLS + b, c * COLS + d) for (a, b), (c, d) in pairs]
    return lax.ppermute(x, ("row", "col"), flat)


def band(offsets, rows, cols):
    pairs = []
    for c in range(COLS):
        for d in offsets:
            r = 2 * c + d
            if 0 <= r < ROWS and 0 <= r + rows < ROWS and 0 <= c + cols < COLS:
                pairs.append(((r, c), (r + rows, c + cols)))
    return pairs


def dot(a, b):
    return jnp.dot(a, b, preferred_element_type=jnp.float32)


def solve(residue, left, right):
    left_vectors, left_inverse, left_values = left
    right_vectors, right_inverse, right_values = right
    first = dot(left_inverse[...], residue.astype(jnp.bfloat16)).astype(jnp.bfloat16)
    second = dot(first, right_vectors[...])
    third = (second / (left_values[...] + right_values[...])).astype(jnp.bfloat16)
    fourth = dot(left_vectors[...], third).astype(jnp.bfloat16)
    return dot(fourth, right_inverse[...])


def tile_of(ref, slot):
    tile = ref.shape[0]
    return ref[:, pl.ds(pl.multiple_of(slot * tile, tile), tile)]


def either(condition, first, second):
    chosen = jnp.where(condition, first.astype(jnp.float32), second.astype(jnp.float32))
    return chosen.astype(jnp.bfloat16)


def first_wave(c, u, p, lam, v, q, mu, x, xb):
    value = solve(c[...], (u, p, lam), (v, q, mu))
    x[...] = value
    xb[...] = value.astype(jnp.bfloat16)


def second_wave(info, c, n, below, across, own, b_wave, u, p, lam, v, q, mu, x, xb):
    slot = info[1]
    left = either(slot == 0, across[...], own[...])
    residue = c[...] - dot(tile_of(n, slot), below[...]) - dot(left, b_wave[...])
    value = solve(residue, (u, p, lam), (v, q, mu))
    x[...] = value
    xb[...] = value.astype(jnp.bfloat16)


def third_wave(
    info, c, a, n, col_two, row_two, col_one, row_one, own, b_two, b_one, u, p, lam, v, q, mu,
    x, *parts,
):
    slot = info[2]
    tile = x.shape[0]
    left = either(slot == 0, row_one[...], own[...])
    a_tile = either(slot == 0, a[:, tile:], n[:, :tile])
    residue = (
        c[...]
        - dot(tile_of(n, slot), col_two[...])
        - dot(row_two[...], b_two[...])
        - dot(a_tile, col_one[...])
        - dot(left, b_one[...])
    )
    value = solve(residue, (u, p, lam), (v, q, mu))
    x[...] = value
    packed = value.astype(jnp.bfloat16)
    across = parts[-1]
    quarter = tile // 4
    for index in range(4):
        rows = slice(index * quarter, (index + 1) * quarter)
        parts[index][0] = packed[rows]
        parts[index][1] = col_one[rows, :]
        parts[index][2] = col_two[rows, :]
    across[0] = packed
    across[1] = left


def last_update(
    info, c, a, n, b, b_above, b_above_two, p_one, p_two, q_one, q_two, across, flipped,
    early, early_flipped,
    x_two, x_one, x_zero, out, down,
):
    tile = c.shape[0]
    piece = p_one.shape[-2]
    a_tiles = (a.at[:, :tile], a.at[:, tile:], n.at[:, :tile], n.at[:, tile:])
    b_tiles = (b, b_above, b_above_two)
    where = info[3]

    @pl.when(where < 1)
    def _():
        for wave in range(3):
            for member in range(2):
                index = member ^ info[4]
                for start, (first, second) in ((0, (p_one, p_two)), (piece, (q_one, q_two))):
                    near = 5 if start == 0 else 9
                    for slot in range(2):
                        at = pl.ds(pl.multiple_of(info[near + slot] * 2 * piece + start, 16), piece)
                        down[member, wave, at, :] = first[slot, index, wave]
                        at = pl.ds(
                            pl.multiple_of(info[near + 2 + slot] * 2 * piece + start, 16), piece
                        )
                        down[member, wave, at, :] = second[slot, index, wave]

    def update(member, source, source_two):
        span = slice(member * tile, (member + 1) * tile)
        change = dot(a_tiles[member][...], down[member, 0])
        for wave in (1, 2):
            change += dot(a_tiles[member + wave][...], down[member, wave])
        for wave in range(2):
            change += dot(source[wave], b_tiles[wave][:, span])
        change += dot(source_two[0], b_tiles[2][:, span])
        out[:, span] = c[:, span] - change

    for member in range(2):
        span = slice(member * tile, (member + 1) * tile)

        @pl.when((where < member) & (info[13] == 0))
        def _():
            update(member, across, early)

        @pl.when((where < member) & (info[13] == 1))
        def _():
            update(member, flipped, early_flipped)

        for wave, solved in enumerate((x_zero, x_one, x_two)):

            @pl.when(where == wave + member)
            def _():
                out[:, span] = solved[...]

        @pl.when(where > 2 + member)
        def _():
            out[:, span] = c[:, span]


def run(name, kernel, outs, dots, info, *operands, scratch=()):
    tile = operands[0].shape[0]
    moved = sum(v.size * v.dtype.itemsize for v in (*operands, *outs))
    whole = pl.BlockSpec(memory_space=pltpu.VMEM)
    scalars = () if info is None else (info,)
    return pl.pallas_call(
        kernel,
        out_shape=outs,
        in_specs=[pl.BlockSpec(memory_space=pltpu.SMEM)] * len(scalars) + [whole] * len(operands),
        out_specs=[whole] * len(outs),
        scratch_shapes=scratch,
        compiler_params=pltpu.CompilerParams(vmem_limit_bytes=GRANT[name] << 20),
        cost_estimate=pl.CostEstimate(
            flops=2 * dots * tile**3, bytes_accessed=moved, transcendentals=0
        ),
    )(*scalars, *operands)


def row_tree(x, offset):
    chips = offset // 2
    for step in (4, 2, 1):
        pairs = []
        for k in range(ROWS):
            for away in range(0, 8, 2 * step):
                c = k // 2 + 2 * away
                if c + 2 * step < COLS:
                    pairs.append(((k, c), (k, c + 2 * step)))
        got = send(x, pairs)
        takes = (offset % 2 == 0) & (chips % (2 * step) == step)
        x = jnp.where(takes, got, x)
    pairs = []
    for k in range(ROWS):
        for c in range(k // 2, COLS, 2):
            if (c ^ 1) > k // 2:
                pairs.append(((k, c), (k, c ^ 1)))
    got = send(x, pairs)
    return x, got


def col_spread(quarters, row, col):
    z = row % 8
    relative = (row // 8) ^ (col // 4)
    diagonal = [(k // 8, k % 8, k // 2) for k in range(ROWS)]
    got = []
    for index, flip in ((1, 1), (2, 3), (3, 2)):
        pairs = [((p * 8 + s, c), ((p ^ flip) * 8 + s, c)) for p, s, c in diagonal]
        got.append(send(quarters[index], pairs))
    part = jnp.where(
        relative == 0,
        quarters[0],
        jnp.where(relative == 1, got[0], jnp.where(relative == 3, got[1], got[2])),
    )
    base = 2 * (col % 4)
    pairs = [((q * 8 + s, c), (q * 8 + 7 - s, c)) for _, s, c in diagonal for q in range(4)]
    got = send(part, pairs)
    part = jnp.where((z // 2) * 2 == base, part, got)
    pairs = []
    for _, s, c in diagonal:
        for q in range(4):
            for t in (s, 7 - s):
                pairs.append(((q * 8 + t, c), (q * 8 + (t ^ 2), c)))
    got = send(part, pairs)
    holds = ((z // 2) * 2 == base) | (((7 - z) // 2) * 2 == base)
    part = jnp.where(holds, part, got)
    every = [(r, c) for r in range(ROWS) for c in range(COLS)]
    got = send(part, [((r, c), (r ^ 1, c)) for r, c in every])
    both = jnp.stack([part, got])
    near = [((r, c), (r ^ 8, c)) for r, c in every]
    far = [((r, c), (r ^ 24, c)) for r, c in every]
    piece = part.shape[1] // 2
    p_one = both[:, :, :piece]
    q_one = both[:, :, piece:]
    p_one = jnp.stack([p_one, send(p_one, near)])
    q_one = jnp.stack([q_one, send(q_one, far)])
    return p_one, send(p_one, far), q_one, send(q_one, near)


def shards(
    c_matrix, a_upper, b_upper, a_vectors, a_inverse, b_vectors, b_inverse, a_values, b_values
):
    tile = a_vectors.shape[1]
    row = lax.axis_index("row")
    col = lax.axis_index("col")
    d = row - 2 * col
    relative = (row // 8) ^ (col // 4)
    z = row % 8
    flips = [relative ^ flip for flip in (0, 1, 3, 2, 0, 3, 1, 2)]
    order = [plane ^ (plane // 2) for plane in flips]
    swapped = (z % 2) ^ ((z // 4) != (col % 4) // 2).astype(jnp.int32)
    parity = jnp.abs(col - row // 2) % 2
    slots = [jnp.clip(d - wave, 0, 1) for wave in (2, 1, 0)]
    info = jnp.stack([*slots, d, swapped, *order, parity])
    c_two, c_one, c_zero = (
        lax.dynamic_slice_in_dim(c_matrix, slot * a_vectors.shape[1], a_vectors.shape[1], 1)
        for slot in slots
    )
    left = (a_vectors, a_inverse, a_values.astype(jnp.float32)[:, None])
    square = jax.ShapeDtypeStruct((tile, tile), jnp.bfloat16)
    exact = jax.ShapeDtypeStruct((tile, tile), jnp.float32)
    strip = jax.ShapeDtypeStruct((3, tile // 4, tile), jnp.bfloat16)
    pair = jax.ShapeDtypeStruct((2, tile, tile), jnp.bfloat16)

    vectors_one = send(b_vectors, band((0, 1), 1, 0))
    inverse_one = send(b_inverse, band((0, 1), 1, 0))
    values_one = send(b_values, band((0, 1), 1, 0))
    vectors_two = send(vectors_one, band((1, 2), 1, 0))
    inverse_two = send(inverse_one, band((1, 2), 1, 0))
    values_two = send(values_one, band((1, 2), 1, 0))
    rights = [
        (vectors, inverse, values.astype(jnp.float32)[None])
        for vectors, inverse, values in (
            (b_vectors, b_inverse, b_values),
            (vectors_one, inverse_one, values_one),
            (vectors_two, inverse_two, values_two),
        )
    ]
    b_tiles = b_upper[:, :tile], b_upper[:, tile:]
    near = jnp.where(d == -1, *b_tiles)
    far = jnp.where(d == -2, *b_tiles)
    b_wave = send(near, band((-1, 0), 2, 0))
    b_one = send(near, band((-1, 0), 1, 0))
    b_two = send(far, band((-2, -1), 2, 0))
    a_next = send(a_upper, [((r, c), (r, c - 1)) for r in range(ROWS) for c in range(1, COLS)])

    def rows_down():
        rows = range(ROWS - 1)
        return [((r, c), (r + 1, c)) for r in rows for c in range(COLS) if r + 1 <= 2 * c]

    b_above = send(b_upper, rows_down())
    b_above_two = send(b_above, rows_down())

    x_two, solved_two = run(
        "K2", first_wave, (exact, square), 4, None,
        c_two.astype(jnp.bfloat16), *left, *rights[2],
    )
    below = send(solved_two, band((2, 3), -1, 0))
    row_two = send(solved_two, band((2, 3), 0, 1))
    col_two = send(solved_two, band((2, 3), -2, 0))
    offset = col - row // 2
    early, early_flipped = row_tree(row_two[None], offset)
    x_one, solved_one = run(
        "K1", second_wave, (exact, square), 6, info,
        c_one, a_next, below, row_two, solved_two, b_wave, *left, *rights[1],
    )
    col_one = send(solved_one, band((1, 2), -1, 0))
    row_one = send(solved_one, band((2,), 0, 1))
    x_zero, *quarters, across = run(
        "K0", third_wave, (exact, *[strip] * 4, pair), 8, info,
        c_zero, a_upper, a_next, col_two, row_two, col_one, row_one, solved_one,
        b_two, b_one, *left, *rights[0],
    )
    pieces = col_spread(quarters, row, col)
    across, flipped = row_tree(across, offset)
    return run(
        "KF", last_update, (jax.ShapeDtypeStruct(c_matrix.shape, jnp.float32),), 12, info,
        c_matrix, a_upper, a_next, b_upper, b_above, b_above_two,
        *pieces, across, flipped, early, early_flipped, x_two, x_one, x_zero,
        scratch=[pltpu.VMEM((2, 3, tile, tile), jnp.bfloat16)],
    )[0]


def solution(mesh):
    placed = (
        P("row", "col"),
        P("row", "col"),
        P("row", "col"),
        P("row", None),
        P("row", None),
        P("row", None),
        P("row", None),
        P("row"),
        P("row"),
    )

    return jax.shard_map(
        shards, mesh=mesh, in_specs=placed, out_specs=P("row", "col"), check_vma=False
    )
```
